32 devices in a mesh: dp: 2 (over core), ctx: 4 (over y, x), tp: 4 (over z).
Axes of the slice: x: 2, y: 2, z: 4, core: 2. Of those that a mesh axis runs over, the one named last changes fastest.
Arguments:
- queries: bfloat16 [4, 8192, 1536], P('dp', 'tp', 'ctx'), may hold values from -6 to 6
- key_proj: bfloat16 [4, 8192, 1536], P('dp', 'tp', 'ctx'), may hold values from -6 to 6
- value_proj: bfloat16 [4, 8192, 1536], P('dp', 'tp', 'ctx'), may hold values from -6 to 6
- grad_output: bfloat16 [4, 8192, 1536], P('dp', 'tp', 'ctx'), may hold values from -6 to 6
- filters: float32 [512, 128], P('tp'), may hold values from -0.5 to 0.5
- group_of: int32 [8192], P('tp'), may hold values from 0 to 511, as said below
Outputs:
- gated_out: bfloat16 [4, 8192, 1536], P('dp', 'tp', 'ctx')
- grad_queries: bfloat16 [4, 8192, 1536], P('dp', 'tp', 'ctx')
- grad_keys: bfloat16 [4, 8192, 1536], P('dp', 'tp', 'ctx')
- grad_values: bfloat16 [4, 8192, 1536], P('dp', 'tp', 'ctx')
- grad_filters: float32 [512, 128], P('tp')
The draws below stay inside these ranges and needn't reach their ends.
Inputs may be any that keep to these rules, and one draw needn't show every extreme that they name: `group_of`: channels come in aligned runs of 16 consecutive channels that share one filter row, and every filter row serves exactly one run.
All inputs are finite; a program needn't handle non-finite values.
Results may differ from the reference program's by a relative error of at most 0.0058.
Values may be sent and summed in bfloat16 or wider, within the bound.
No kernel may reach another device: no remote copies, remote signals or barrier semaphores. Data moves between devices by JAX's collectives and lax.ppermute only.
A program may use at most 192 MiB of HBM per device.

```python
import jax
import jax.numpy as jnp
from jax import lax

D = 8192
GROUPS = 512
TAPS = 128
LENGTH = 1536
BATCH = 4
TOKENS = 6144


def draw_group_of(key, part):
    filter_order = jax.random.permutation(key, GROUPS)
    return jnp.repeat(filter_order, D // GROUPS).astype(jnp.int32)


def shard_levels(stream_key, dims, cuts, smallest, high):
    factor_of = 1.0
    for dim, parts in cuts:
        draws = jax.random.uniform(jax.random.fold_in(jax.random.fold_in(stream_key, 6), dim), (parts,), jnp.float32, smallest / len(cuts), high / len(cuts))
        factor_of = factor_of * jnp.repeat(jnp.exp(draws), dims[dim] // parts).reshape((-1,) + (1,) * (len(dims) - 1 - dim))
    return factor_of


def scatter_about(own_key, shape, spread, bound, pieces=(), kind=jnp.bfloat16):
    values = jax.random.normal(own_key, shape, jnp.float32) * spread
    if len(pieces) > 0:
        values = shard_levels(own_key, shape, pieces, -0.22, 0.18) * values
    return jnp.clip(values, min=-bound, max=bound).astype(kind)


def setup_inputs(seed: int = 0) -> dict:
    key_list = jax.random.split(jax.random.key(seed), 7)
    queries = scatter_about(key_list[0], (BATCH, D, LENGTH), 1.0, 6.0, ((0, 2), (1, 4), (2, 4)))
    key_proj = scatter_about(key_list[1], (BATCH, D, LENGTH), 1.0, 6.0, ((0, 2), (1, 4), (2, 4)))
    value_proj = scatter_about(key_list[2], (BATCH, D, LENGTH), 1.0, 6.0, ((0, 2), (1, 4), (2, 4)))
    grad_output = scatter_about(key_list[3], (BATCH, D, LENGTH), 1.0, 6.0, ((0, 2), (1, 4), (2, 4)))
    filters = scatter_about(key_list[4], (GROUPS, TAPS), TAPS ** -0.5, 0.5, ((0, 4),), jnp.float32)
    group_of = draw_group_of(jax.random.fold_in(key_list[6], 71), 0)
    return dict(queries=queries, key_proj=key_proj, value_proj=value_proj, grad_output=grad_output, filters=filters, group_of=group_of)


def reference(queries, key_proj, value_proj, grad_output, filters, group_of):
    wide = jnp.float32
    rounded = lax.optimization_barrier(filters.astype(jnp.bfloat16))
    filter_table = rounded.astype(wide)
    chan_taps_all = filter_table[group_of]
    block_width = min(D, 512)
    block_count = D // block_width
    fft_len = LENGTH + TAPS

    def one_window(window_pos):
        def select_row(array):
            return lax.dynamic_index_in_dim(array, window_pos, 0, keepdims=False)

        q_rows = select_row(queries)
        k_rows = select_row(key_proj)
        v_rows = select_row(value_proj)
        g_rows = select_row(grad_output)

        def one_block(block_pos):
            first_row = block_pos * block_width

            def cut_rows(array):
                return lax.dynamic_slice_in_dim(array, first_row, block_width, 0).astype(wide)

            q_block = cut_rows(q_rows)
            k_block = cut_rows(k_rows)
            v_block = cut_rows(v_rows)
            g_block = cut_rows(g_rows)
            chan_taps = lax.dynamic_slice_in_dim(chan_taps_all, first_row, block_width, 0)
            product = lax.optimization_barrier((k_block * v_block).astype(jnp.bfloat16)).astype(wide)
            backward = lax.optimization_barrier((g_block * q_block).astype(jnp.bfloat16)).astype(wide)
            spec_prod = jnp.fft.rfft(product, n=fft_len, axis=1)
            spec_taps = jnp.fft.rfft(chan_taps, n=fft_len, axis=1)
            spec_back = jnp.fft.rfft(backward, n=fft_len, axis=1)
            mixed_rows = jnp.fft.irfft(spec_prod * spec_taps, n=fft_len, axis=1)[:, :LENGTH].astype(wide)
            upward = jnp.fft.irfft(spec_back * jnp.conj(spec_taps), n=fft_len, axis=1)[:, :LENGTH].astype(wide)
            tap_grad = jnp.fft.irfft(spec_back * jnp.conj(spec_prod), n=fft_len, axis=1)[:, :TAPS].astype(wide)
            return ((q_block * mixed_rows).astype(jnp.bfloat16),
                    (g_block * mixed_rows).astype(jnp.bfloat16),
                    (upward * v_block).astype(jnp.bfloat16),
                    (upward * k_block).astype(jnp.bfloat16),
                    tap_grad)

        results = lax.map(one_block, jnp.arange(block_count, dtype=jnp.int32))

        def join_rows(stacked):
            return stacked.reshape(D, LENGTH)

        chan_grad = results[4].reshape(D, TAPS)
        return (join_rows(results[0]), join_rows(results[1]), join_rows(results[2]), join_rows(results[3]), chan_grad)

    gated_out, grad_queries, grad_keys, grad_values, chan_grads = lax.map(one_window, jnp.arange(BATCH, dtype=jnp.int32))
    summed = jnp.sum(chan_grads, axis=0)
    grad_filters = jax.ops.segment_sum(summed, group_of, num_segments=GROUPS) / TOKENS
    return gated_out, grad_queries, grad_keys, grad_values, grad_filters
```

```python
import jax
import jax.numpy as jnp
from jax import lax
from jax.experimental import pallas as pl
from jax.experimental.pallas import tpu as pltpu
from jax.sharding import PartitionSpec as P

WIDE = jnp.float32
NARROW = jnp.bfloat16


def wide_dot(left, right, left_dim, right_dim):
    return lax.dot_general(
        left, right, (((left_dim,), (right_dim,)), ((), ())), preferred_element_type=WIDE
    )


def product(left, right):
    return (left.astype(WIDE) * right.astype(WIDE)).astype(NARROW)


def causal_mask(taps):
    row = lax.broadcasted_iota(jnp.int32, (taps, taps), 0)
    lane = lax.broadcasted_iota(jnp.int32, (taps, taps), 1)
    return lane >= row


def banded(filter_row, mask, own_first):
    taps = filter_row.shape[1]
    spread = jnp.broadcast_to(filter_row, (taps, taps))
    circulant = pltpu.roll(spread, 0, 1, stride=1, stride_axis=0)
    kept = jnp.where(mask, circulant, 0.0).astype(NARROW)
    rest = jnp.where(mask, 0.0, circulant).astype(NARROW)
    return kept, rest


def diagonal_sum(square):
    taps = square.shape[0]
    total = square[:8]
    for a in range(8, taps, 8):
        total = total + pltpu.roll(square[a : a + 8], taps - a, 1)
    row = lax.broadcasted_iota(jnp.int32, total.shape, 0)
    for bit in (1, 2, 4):
        total = jnp.where(row & bit != 0, pltpu.roll(total, taps - bit, 1), total)
    return jnp.sum(total, axis=0, keepdims=True)


def interior_kernel(
    tp_size, members, ids_ref, *refs
):
    pieces = refs[:tp_size]
    q_ref, k_ref, v_ref, g_ref = refs[tp_size : tp_size + 4]
    gated_ref, gq_ref, gk_ref, gv_ref, grad_ref, h_ref, hr_ref = refs[tp_size + 4 :]
    taps = h_ref.shape[1]
    windows, channels, positions = q_ref.shape
    blocks = positions // taps
    step = pl.program_id(0)

    @pl.when(step == 0)
    def _():
        me = lax.axis_index("tp")
        owned = pieces[0].shape[0]
        group = lax.broadcasted_iota(jnp.int32, (owned, h_ref.shape[0]), 0)
        total = jnp.zeros(h_ref.shape, WIDE)
        for k in range(tp_size):
            source = lax.rem(me + tp_size - k, tp_size)
            chosen = (group + source * owned == ids_ref[...]).astype(WIDE).astype(NARROW)
            total = total + wide_dot(chosen, pieces[k][...], 0, 0)
        h_ref[...] = total
        row = lax.broadcasted_iota(jnp.int32, (taps, taps), 0)
        lane = lax.broadcasted_iota(jnp.int32, (taps, taps), 1)
        turn = (lax.rem(row + lane, taps) == 0).astype(WIDE).astype(NARROW)
        hr_ref[...] = wide_dot(total.astype(NARROW), turn, 1, 0)

    mask = causal_mask(taps)
    reverse_mask = jnp.logical_not(causal_mask(taps)) | (
        lax.broadcasted_iota(jnp.int32, (taps, taps), 0)
        == lax.broadcasted_iota(jnp.int32, (taps, taps), 1)
    )
    groups = channels // members
    for r in range(groups):
        rows = slice(r * members, (r + 1) * members)
        base = step * groups
        h_row = h_ref[pl.ds(base + r, 1), :]
        hr_row = hr_ref[pl.ds(base + r, 1), :]
        own, prior = banded(h_row, mask, True)
        own_t, prior_t = banded(hr_row, reverse_mask, True)
        forward = jnp.concatenate([prior, own], axis=0)
        backward = jnp.concatenate([own_t, prior_t], axis=0)
        u_rows, d_rows, z_in, du_in = [], [], [], []
        u_outer, d_outer = [], []
        for w in range(windows):
            u = product(k_ref[w, rows, :], v_ref[w, rows, :])
            d = product(q_ref[w, rows, :], g_ref[w, rows, :])
            for b in range(blocks):
                d_outer.append(d[:, b * taps : (b + 1) * taps])
                if b == 0:
                    u_outer.append(
                        jnp.concatenate([jnp.zeros((members, taps), NARROW), u[:, :taps]], axis=1)
                    )
                else:
                    u_outer.append(u[:, (b - 1) * taps : (b + 1) * taps])
                if b > 0:
                    z_in.append(u[:, (b - 1) * taps : (b + 1) * taps])
                if b < blocks - 1:
                    du_in.append(d[:, b * taps : (b + 2) * taps])
        z = wide_dot(jnp.concatenate(z_in, axis=0), forward, 1, 0)
        du = wide_dot(jnp.concatenate(du_in, axis=0), backward, 1, 0)
        outer = wide_dot(
            jnp.concatenate(u_outer, axis=0), jnp.concatenate(d_outer, axis=0), 0, 0
        )
        square = jnp.where(mask, outer[taps:], outer[:taps])
        grad_ref[r : r + 1, :] = diagonal_sum(square)
        at = 0
        for w in range(windows):
            for b in range(1, blocks):
                cols = slice(b * taps, (b + 1) * taps)
                part = z[at * members : (at + 1) * members]
                gated_ref[w, rows, cols] = (q_ref[w, rows, cols].astype(WIDE) * part).astype(NARROW)
                gq_ref[w, rows, cols] = (g_ref[w, rows, cols].astype(WIDE) * part).astype(NARROW)
                cols = slice((b - 1) * taps, b * taps)
                part = du[at * members : (at + 1) * members]
                gk_ref[w, rows, cols] = (v_ref[w, rows, cols].astype(WIDE) * part).astype(NARROW)
                gv_ref[w, rows, cols] = (k_ref[w, rows, cols].astype(WIDE) * part).astype(NARROW)
                at += 1


def interior(ids, pieces, queries, key_proj, value_proj, grad_output, members):
    windows, channels, positions = queries.shape
    taps = pieces[0].shape[1]
    here = channels // members
    step_groups = 8
    block = step_groups * members
    steps = channels // block
    wide_spec = pl.BlockSpec((windows, block, positions), lambda i: (0, i, 0))
    whole = lambda shape: pl.BlockSpec(shape, lambda i: (0,) * len(shape))
    big = jax.ShapeDtypeStruct(queries.shape, NARROW)
    table = jax.ShapeDtypeStruct((here, taps), WIDE)
    nbytes = queries.size * 2

    def kernel(*refs):
        interior_kernel(len(pieces), members, *refs)

    return pl.pallas_call(
        kernel,
        grid=(steps,),
        in_specs=[whole(ids.shape)] + [whole(p.shape) for p in pieces] + [wide_spec] * 4,
        out_specs=[wide_spec] * 4
        + [pl.BlockSpec((step_groups, taps), lambda i: (i, 0)), whole(table.shape), whole(table.shape)],
        out_shape=[big] * 4 + [table] * 3,
        cost_estimate=pl.CostEstimate(flops=20 * nbytes * 128, bytes_accessed=8 * nbytes, transcendentals=0),
        name="interior",
    )(ids, *pieces, queries, key_proj, value_proj, grad_output)


def cross_kernel(members, scale, x_ref, d_ref, q_ref, g_ref, k_ref, v_ref, grad_ref, out_ref):
    even = lax.rem(lax.axis_index("ctx"), 2) == 0
    taps = x_ref.shape[-1]
    mask = causal_mask(taps)
    half, channels = x_ref.shape[:2]
    for r in range(channels // members):
        rows = slice(r * members, (r + 1) * members)
        lefts, rights = [], []
        for w in range(half):
            x, d = x_ref[w, rows, :], d_ref[w, rows, :]
            lefts.append(jnp.where(even, d, x))
            rights.append(product(q_ref[w, rows, :], g_ref[w, rows, :]))
            lefts.append(product(k_ref[w, rows, :], v_ref[w, rows, :]))
            rights.append(jnp.where(even, x, d))
        outer = wide_dot(jnp.concatenate(lefts, axis=0), jnp.concatenate(rights, axis=0), 0, 0)
        square = jnp.where(mask, 0.0, outer)
        out_ref[r : r + 1, :] = (grad_ref[r : r + 1, :] + diagonal_sum(square)) * scale


def cross_terms(x1, d1, queries, key_proj, value_proj, grad_output, grad, members, scale):
    windows, channels, positions = queries.shape
    taps = grad.shape[1]
    half = x1.shape[0]
    step_groups = 16
    block = step_groups * members
    last = positions // taps - 1
    halo = pl.BlockSpec((half, block, taps), lambda i: (0, i, 0))
    head = pl.BlockSpec((half, block, taps), lambda i: (0, i, 0))
    tail = pl.BlockSpec((half, block, taps), lambda i: (1, i, last))
    rows = pl.BlockSpec((step_groups, taps), lambda i: (i, 0))

    def kernel(*refs):
        cross_kernel(members, scale, *refs)

    return pl.pallas_call(
        kernel,
        grid=(channels // block,),
        in_specs=[halo, halo, head, head, tail, tail, rows],
        out_specs=rows,
        out_shape=jax.ShapeDtypeStruct(grad.shape, WIDE),
        cost_estimate=pl.CostEstimate(flops=x1.size * 512, bytes_accessed=12 * x1.size, transcendentals=0),
        name="cross",
    )(x1, d1, queries, grad_output, key_proj, value_proj, grad)


def border_kernel(members, *refs):
    (x1_ref, d1_ref, x2_ref, d2_ref, h_ref, hr_ref) = refs[:6]
    qh_ref, gh_ref, kh_ref, vh_ref, qt_ref, gt_ref, kt_ref, vt_ref = refs[6:14]
    gated_ref, gq_ref, gk_ref, gv_ref = refs[18:]
    even = lax.rem(lax.axis_index("ctx"), 2) == 0
    taps = x1_ref.shape[-1]
    mask = causal_mask(taps)
    reverse_mask = jnp.logical_not(mask) | (
        lax.broadcasted_iota(jnp.int32, (taps, taps), 0)
        == lax.broadcasted_iota(jnp.int32, (taps, taps), 1)
    )
    half, channels = x1_ref.shape[:2]
    for r in range(channels // members):
        rows = slice(r * members, (r + 1) * members)
        own, prior = banded(h_ref[r : r + 1, :], mask, True)
        own_t, prior_t = banded(hr_ref[r : r + 1, :], reverse_mask, True)
        forward = jnp.concatenate([prior, own], axis=0)
        backward = jnp.concatenate([own_t, prior_t], axis=0)
        z_in, du_in = [], []
        for first in (True, False):
            for w in range(half):
                x = (x1_ref if first else x2_ref)[w, rows, :]
                d = (d1_ref if first else d2_ref)[w, rows, :]
                at = w if first else w + half
                z_in.append(
                    jnp.concatenate(
                        [jnp.where(even, d, x), product(kh_ref[at, rows, :], vh_ref[at, rows, :])], axis=1
                    )
                )
                at = w + half if first else w
                du_in.append(
                    jnp.concatenate(
                        [product(qt_ref[at, rows, :], gt_ref[at, rows, :]), jnp.where(even, x, d)], axis=1
                    )
                )
        z = wide_dot(jnp.concatenate(z_in, axis=0), forward, 1, 0)
        du = wide_dot(jnp.concatenate(du_in, axis=0), backward, 1, 0)
        for w in range(2 * half):
            part = z[w * members : (w + 1) * members]
            gated_ref[w, rows, :] = (qh_ref[w, rows, :].astype(WIDE) * part).astype(NARROW)
            gq_ref[w, rows, :] = (gh_ref[w, rows, :].astype(WIDE) * part).astype(NARROW)
            at = (w + half) % (2 * half)
            part = du[w * members : (w + 1) * members]
            gk_ref[at, rows, :] = (vt_ref[at, rows, :].astype(WIDE) * part).astype(NARROW)
            gv_ref[at, rows, :] = (kt_ref[at, rows, :].astype(WIDE) * part).astype(NARROW)


def border(x1, d1, x2, d2, h, hr, queries, key_proj, value_proj, grad_output, outs, members):
    windows, channels, positions = queries.shape
    taps = h.shape[1]
    half = x1.shape[0]
    step_groups = 16
    block = step_groups * members
    last = positions // taps - 1
    halo = pl.BlockSpec((half, block, taps), lambda i: (0, i, 0))
    head = pl.BlockSpec((windows, block, taps), lambda i: (0, i, 0))
    tail = pl.BlockSpec((windows, block, taps), lambda i: (0, i, last))
    rows = pl.BlockSpec((step_groups, taps), lambda i: (i, 0))
    anywhere = pl.BlockSpec(memory_space=pl.ANY)

    def kernel(*refs):
        border_kernel(members, *refs)

    return pl.pallas_call(
        kernel,
        grid=(channels // block,),
        in_specs=[halo] * 4 + [rows] * 2 + [head] * 4 + [tail] * 4 + [anywhere] * 4,
        out_specs=[head, head, tail, tail],
        out_shape=[jax.ShapeDtypeStruct(queries.shape, NARROW)] * 4,
        input_output_aliases={14: 0, 15: 1, 16: 2, 17: 3},
        cost_estimate=pl.CostEstimate(flops=x1.size * 2048, bytes_accessed=32 * x1.size, transcendentals=0),
        name="border",
    )(
        x1, d1, x2, d2, h, hr,
        queries, grad_output, key_proj, value_proj,
        queries, grad_output, key_proj, value_proj,
        *outs,
    )


def place_kernel(ids_refs, rows_ref, out_ref):
    me = lax.axis_index("tp")
    tp_size = len(ids_refs)
    owned, taps = out_ref.shape
    slices, _, each, _ = rows_ref.shape
    total = jnp.zeros(out_ref.shape, WIDE)
    for k in range(tp_size):
        source = lax.rem(me + tp_size - k, tp_size)
        ids = ids_refs[k][...].astype(WIDE)
        number = (ids[0:1, :] * 256.0 + ids[1:2, :]).astype(jnp.int32)
        here = number.shape[1]
        slot = lax.broadcasted_iota(jnp.int32, (owned, here), 0) + me * owned
        chosen = (slot == number).astype(WIDE).astype(NARROW)
        piece = rows_ref[:, pl.ds(source, 1)].reshape(slices * each, taps)
        total = total + wide_dot(chosen, piece, 1, 0)
    out_ref[...] = total


def shards(queries, key_proj, value_proj, grad_output, filters, group_of):
    windows, channels, positions = queries.shape
    owned, taps = filters.shape
    ctx_size, tp_size, dp_size = (lax.axis_size(a) for a in ("ctx", "tp", "dp"))
    members = channels // owned
    half = windows // 2
    even = lax.rem(lax.axis_index("ctx"), 2) == 0

    def messages(u_at, d_at):
        u = product(key_proj[u_at : u_at + half, :, -taps:], value_proj[u_at : u_at + half, :, -taps:])
        d = product(queries[d_at : d_at + half, :, :taps], grad_output[d_at : d_at + half, :, :taps])
        return jnp.where(even, u, d), jnp.where(even, d, u)

    every = range(ctx_size)
    near = [(i, i ^ 1) for i in every]
    far = [(i, i + 1) for i in every if i % 2 == 1 and i + 1 < ctx_size]
    far += [(i, i - 1) for i in every if i % 2 == 0 and i > 0]
    out_hop = [(i, i + 2) for i in every if i % 2 == 1 and i + 1 < ctx_size]
    out_hop += [(i, i - 2) for i in every if i % 2 == 0 and i > 0]
    back_hop = [(i + 2, i + 1) for i in every if i % 2 == 1 and i + 1 < ctx_size]
    back_hop += [(i - 2, i - 1) for i in every if i % 2 == 0 and i > 0]
    near_1, far_1 = messages(0, half)
    near_2, far_2 = messages(half, 0)
    x1 = lax.ppermute(near_1, "ctx", near)
    d1 = lax.ppermute(far_1, "ctx", far)
    x2 = lax.ppermute(near_2, "ctx", near)
    relay = lax.ppermute(far_2, "ctx", out_hop)
    d2 = lax.ppermute(relay, "ctx", back_hop)

    run_ids = group_of.reshape(1, owned, members)[:, :, 0]
    id_rows = jnp.concatenate(
        [run_ids // 256, run_ids % 256, jnp.zeros((14, owned), jnp.int32)], axis=0
    ).astype(NARROW)
    sent = jnp.concatenate([filters.astype(NARROW), id_rows], axis=0)
    heard = [sent]
    for k in range(1, tp_size):
        heard.append(lax.ppermute(sent, "tp", [(i, (i + k) % tp_size) for i in range(tp_size)]))
    pieces = [p[:owned] for p in heard]
    ids = [p[owned:] for p in heard]

    *outs, grad, h, hr = interior(run_ids, pieces, queries, key_proj, value_proj, grad_output, members)
    scale = 1.0 / (windows * positions * dp_size * ctx_size)
    grad = cross_terms(x1, d1, queries, key_proj, value_proj, grad_output, grad, members, scale)
    outs = border(x1, d1, x2, d2, h, hr, queries, key_proj, value_proj, grad_output, outs, members)

    slices = dp_size * ctx_size
    each = owned // slices
    swapped = lax.all_to_all(grad, ("dp", "ctx"), 0, 0, tiled=True)
    summed = jnp.sum(swapped.reshape(slices, each, taps), axis=0).astype(NARROW)
    copies = jnp.broadcast_to(summed[None], (slices * tp_size, each, taps))
    rows = lax.all_to_all(copies, ("dp", "ctx", "tp"), 0, 0, tiled=True)
    rows = rows.reshape(slices, tp_size, each, taps)

    def kernel(*refs):
        place_kernel(refs[:tp_size], refs[tp_size], refs[tp_size + 1])

    grad_filters = pl.pallas_call(
        kernel, out_shape=jax.ShapeDtypeStruct((owned, taps), WIDE), name="place"
    )(*ids, rows)
    return (*outs, grad_filters)


def solution(mesh):
    data = P("dp", "tp", "ctx")
    in_specs = (data, data, data, data, P("tp", None), P("tp"))
    out_specs = (data, data, data, data, P("tp", None))
    return jax.shard_map(shards, mesh=mesh, in_specs=in_specs, out_specs=out_specs, check_vma=False)
```

```python
import jax
import jax.numpy as jnp
from jax import lax
from jax.experimental import pallas as pl
from jax.experimental.pallas import tpu as pltpu
from jax.sharding import PartitionSpec as P

WIDE = jnp.float32
NARROW = jnp.bfloat16


def wide_dot(left, right, left_dim, right_dim):
    return lax.dot_general(
        left, right, (((left_dim,), (right_dim,)), ((), ())), preferred_element_type=WIDE
    )


def circulant(filter_row):
    taps = filter_row.shape[1]
    spread = jnp.broadcast_to(filter_row, (taps, taps))
    return pltpu.roll(spread, 0, 1, stride=1, stride_axis=0)


def band_weights(h_row, hr_row):
    taps = h_row.shape[1]
    row = lax.broadcasted_iota(jnp.int32, (taps, taps), 0)
    lane = lax.broadcasted_iota(jnp.int32, (taps, taps), 1)
    turned = circulant(h_row)
    own = jnp.where(lane >= row, turned, 0.0).astype(NARROW)
    earlier = jnp.where(lane >= row, 0.0, turned).astype(NARROW)
    turned = circulant(hr_row)
    own_back = jnp.where(lane <= row, turned, 0.0).astype(NARROW)
    later = jnp.where(lane <= row, 0.0, turned).astype(NARROW)
    return jnp.concatenate([earlier, own], axis=0), jnp.concatenate([own_back, later], axis=0)


def diagonal_sum(square):
    taps = square.shape[0]
    total = square[:8]
    for a in range(8, taps, 8):
        total = total + pltpu.roll(square[a : a + 8], taps - a, 1)
    row = lax.broadcasted_iota(jnp.int32, total.shape, 0)
    for bit in (1, 2, 4):
        total = jnp.where(row & bit != 0, pltpu.roll(total, taps - bit, 1), total)
    return jnp.sum(total, axis=0, keepdims=True)


def conv_kernel(tp_size, owned, members, ids_ref, *refs):
    pieces = refs[:tp_size]
    q_ref, k_ref, v_ref, g_ref = refs[tp_size : tp_size + 4]
    gated_ref, gq_ref, gk_ref, gv_ref, h_ref, hr_ref, near_ref, far_ref = refs[tp_size + 4 :]
    even = lax.rem(lax.axis_index("ctx"), 2) == 0
    taps = h_ref.shape[1]
    windows, channels, positions = q_ref.shape
    blocks = positions // taps
    half = windows // 2
    step = pl.program_id(0)

    @pl.when(step == 0)
    def _():
        me = lax.axis_index("tp")
        group = lax.broadcasted_iota(jnp.int32, (owned, h_ref.shape[0]), 0)
        total = jnp.zeros(h_ref.shape, WIDE)
        for k in range(tp_size):
            source = lax.rem(me + tp_size - k, tp_size)
            chosen = (group + source * owned == ids_ref[...]).astype(WIDE).astype(NARROW)
            total = total + wide_dot(chosen, pieces[k][:owned, :], 0, 0)
        h_ref[...] = total
        row = lax.broadcasted_iota(jnp.int32, (taps, taps), 0)
        lane = lax.broadcasted_iota(jnp.int32, (taps, taps), 1)
        turn = (lax.rem(row + lane, taps) == 0).astype(WIDE).astype(NARROW)
        hr_ref[...] = wide_dot(total.astype(NARROW), turn, 1, 0)

    groups = channels // members
    for r in range(groups):
        rows = slice(r * members, (r + 1) * members)
        at = step * groups + r
        forward, backward = band_weights(h_ref[pl.ds(at, 1), :], hr_ref[pl.ds(at, 1), :])
        z_in, du_in, u_ends, d_ends = [], [], [], []
        for w in range(windows):
            u = k_ref[w, rows, :] * v_ref[w, rows, :]
            d = q_ref[w, rows, :] * g_ref[w, rows, :]
            if w < half:
                d_ends.append(d[:, :taps])
            else:
                u_ends.append(u[:, -taps:])
            for b in range(1, blocks):
                z_in.append(u[:, (b - 1) * taps : (b + 1) * taps])
                du_in.append(d[:, (b - 1) * taps : (b + 1) * taps])
        z = wide_dot(jnp.concatenate(z_in, axis=0), forward, 1, 0).astype(NARROW)
        du = wide_dot(jnp.concatenate(du_in, axis=0), backward, 1, 0).astype(NARROW)
        for w in range(half):
            near_ref[w, rows, :] = jnp.where(even, u_ends[w], d_ends[w])
            far_ref[w, rows, :] = jnp.where(even, d_ends[w], u_ends[w])
        at = 0
        for w in range(windows):
            for b in range(1, blocks):
                cols = slice(b * taps, (b + 1) * taps)
                part = z[at * members : (at + 1) * members]
                gated_ref[w, rows, cols] = q_ref[w, rows, cols] * part
                gq_ref[w, rows, cols] = g_ref[w, rows, cols] * part
                cols = slice((b - 1) * taps, b * taps)
                part = du[at * members : (at + 1) * members]
                gk_ref[w, rows, cols] = v_ref[w, rows, cols] * part
                gv_ref[w, rows, cols] = k_ref[w, rows, cols] * part
                at += 1


def whole_spec(shape):
    return pl.BlockSpec(shape, lambda i: (0,) * len(shape))


def conv(ids, heard, owned, queries, key_proj, value_proj, grad_output, members, step_groups=32):
    windows, channels, positions = queries.shape
    half = windows // 2
    taps = heard[0].shape[1]
    here = channels // members
    block = step_groups * members
    vmem = pl.BlockSpec(memory_space=pltpu.VMEM)
    wide_spec = pl.BlockSpec((windows, block, positions), lambda i: (0, i, 0))
    halo = pl.BlockSpec((half, block, taps), lambda i: (0, i, 0))
    big = jax.ShapeDtypeStruct(queries.shape, NARROW)
    table = jax.ShapeDtypeStruct((here, taps), WIDE)
    ends = jax.ShapeDtypeStruct((half, channels, taps), NARROW)

    def kernel(*refs):
        conv_kernel(len(heard), owned, members, *refs)

    return pl.pallas_call(
        kernel,
        grid=(channels // block,),
        in_specs=[vmem] * (1 + len(heard)) + [wide_spec] * 4,
        out_specs=[wide_spec] * 4 + [whole_spec(table.shape)] * 2 + [halo] * 2,
        out_shape=[big] * 4 + [table] * 2 + [ends] * 2,
        cost_estimate=pl.CostEstimate(
            flops=8 * taps * queries.size, bytes_accessed=16 * queries.size, transcendentals=0
        ),
        name="conv",
    )(ids, *heard, queries, key_proj, value_proj, grad_output)


def outer_kernel(members, scale, chunk, x_ref, d_ref, q_ref, k_ref, v_ref, g_ref, _, out_ref, square_ref):
    even = lax.rem(lax.axis_index("ctx"), 2) == 0
    windows, channels, positions = q_ref.shape
    half = windows // 2
    taps = x_ref.shape[-1]
    first = pl.program_id(0) * channels
    blocks = positions // taps
    chunks = channels // members // chunk
    slots = square_ref.shape[0]
    row = lax.broadcasted_iota(jnp.int32, (taps, taps), 0)
    lane = lax.broadcasted_iota(jnp.int32, (taps, taps), 1)
    empty = jnp.zeros((members, taps), NARROW)

    def squares(at, slot):
        for r in range(chunk):
            rows = slice((at * chunk + r) * members, (at * chunk + r + 1) * members)
            halo_rows = pl.ds(pl.multiple_of(first + (at * chunk + r) * members, members), members)
            lefts, rights = [], []
            for w in range(windows):
                u = k_ref[w, rows, :] * v_ref[w, rows, :]
                d = q_ref[w, rows, :] * g_ref[w, rows, :]
                if w < half:
                    prior = jnp.where(even, d_ref[w, halo_rows, :], x_ref[w, halo_rows, :])
                else:
                    prior = empty
                    lefts.append(
                        jnp.where(even, x_ref[w - half, halo_rows, :], d_ref[w - half, halo_rows, :])
                    )
                    rights.append(jnp.concatenate([u[:, -taps:], empty], axis=1))
                for b in range(blocks):
                    lefts.append(d[:, b * taps : (b + 1) * taps])
                    if b == 0:
                        rights.append(jnp.concatenate([prior, u[:, :taps]], axis=1))
                    else:
                        rights.append(u[:, (b - 1) * taps : (b + 1) * taps])
            outer = wide_dot(jnp.concatenate(lefts, axis=0), jnp.concatenate(rights, axis=0), 0, 0)
            square_ref[slot, r] = jnp.where(lane <= row, outer[:, taps:], outer[:, :taps])

    def sums(at, slot):
        found = [diagonal_sum(square_ref[slot, r]) for r in range(chunk)]
        out_ref[at * chunk : (at + 1) * chunk, :] = jnp.concatenate(found, axis=0) * scale

    for at in range(chunks + 1):
        if at < chunks:
            squares(at, at % slots)
        if at > 0:
            sums(at - 1, (at - 1) % slots)


def outer_terms(x1, d1, after, queries, key_proj, value_proj, grad_output, members, scale, step_groups=16, chunk=8, slots=2):
    windows, channels, positions = queries.shape
    taps = x1.shape[-1]
    block = step_groups * members
    vmem = pl.BlockSpec(memory_space=pltpu.VMEM)
    wide_spec = pl.BlockSpec((windows, block, positions), lambda i: (0, i, 0))

    def kernel(*refs):
        outer_kernel(members, scale, chunk, *refs)

    return pl.pallas_call(
        kernel,
        grid=(channels // block,),
        in_specs=[vmem, vmem] + [wide_spec] * 4 + [pl.BlockSpec(memory_space=pl.ANY)],
        out_specs=pl.BlockSpec((step_groups, taps), lambda i: (i, 0)),
        out_shape=jax.ShapeDtypeStruct((channels // members, taps), WIDE),
        scratch_shapes=[pltpu.VMEM((slots, chunk, taps, taps), WIDE)],
        cost_estimate=pl.CostEstimate(
            flops=8 * taps * queries.size, bytes_accessed=8 * queries.size, transcendentals=0
        ),
        name="outer",
    )(x1, d1, queries, key_proj, value_proj, grad_output, after)


def border_kernel(members, *refs):
    (x1_ref, d1_ref, x2_ref, d2_ref, h_ref, hr_ref) = refs[:6]
    qh_ref, gh_ref, kh_ref, vh_ref, qt_ref, gt_ref, kt_ref, vt_ref = refs[6:14]
    gated_ref, gq_ref, gk_ref, gv_ref = refs[18:]
    even = lax.rem(lax.axis_index("ctx"), 2) == 0
    half, _, taps = x1_ref.shape
    channels = qh_ref.shape[1]
    start = pl.program_id(0) * channels
    for r in range(channels // members):
        rows = slice(r * members, (r + 1) * members)
        halo_rows = pl.ds(pl.multiple_of(start + r * members, members), members)
        forward, backward = band_weights(h_ref[r : r + 1, :], hr_ref[r : r + 1, :])
        z_in, du_in = [], []
        for w in range(2 * half):
            first = w < half
            x = (x1_ref if first else x2_ref)[w % half, halo_rows, :]
            d = (d1_ref if first else d2_ref)[w % half, halo_rows, :]
            z_in.append(
                jnp.concatenate([jnp.where(even, d, x), kh_ref[w, rows, :] * vh_ref[w, rows, :]], axis=1)
            )
            x = (x2_ref if first else x1_ref)[w % half, halo_rows, :]
            d = (d2_ref if first else d1_ref)[w % half, halo_rows, :]
            du_in.append(
                jnp.concatenate([qt_ref[w, rows, :] * gt_ref[w, rows, :], jnp.where(even, x, d)], axis=1)
            )
        z = wide_dot(jnp.concatenate(z_in, axis=0), forward, 1, 0).astype(NARROW)
        du = wide_dot(jnp.concatenate(du_in, axis=0), backward, 1, 0).astype(NARROW)
        for w in range(2 * half):
            part = z[w * members : (w + 1) * members]
            gated_ref[w, rows, :] = qh_ref[w, rows, :] * part
            gq_ref[w, rows, :] = gh_ref[w, rows, :] * part
            part = du[w * members : (w + 1) * members]
            gk_ref[w, rows, :] = vt_ref[w, rows, :] * part
            gv_ref[w, rows, :] = kt_ref[w, rows, :] * part


def border(x1, d1, x2, d2, h, hr, queries, key_proj, value_proj, grad_output, outs, members, step_groups=64):
    windows, channels, positions = queries.shape
    taps = x1.shape[-1]
    block = step_groups * members
    last = positions // taps - 1
    halo = pl.BlockSpec(memory_space=pltpu.VMEM)
    head = pl.BlockSpec((windows, block, taps), lambda i: (0, i, 0))
    tail = pl.BlockSpec((windows, block, taps), lambda i: (0, i, last))
    rows = pl.BlockSpec((step_groups, taps), lambda i: (i, 0))
    anywhere = pl.BlockSpec(memory_space=pl.ANY)

    def kernel(*refs):
        border_kernel(members, *refs)

    return pl.pallas_call(
        kernel,
        grid=(channels // block,),
        in_specs=[halo] * 4 + [rows] * 2 + [head] * 4 + [tail] * 4 + [anywhere] * 4,
        out_specs=[head, head, tail, tail],
        out_shape=[jax.ShapeDtypeStruct(queries.shape, NARROW)] * 4,
        input_output_aliases={14: 0, 15: 1, 16: 2, 17: 3},
        cost_estimate=pl.CostEstimate(
            flops=32 * taps * x1.size, bytes_accessed=64 * x1.size, transcendentals=0
        ),
        name="border",
    )(
        x1, d1, x2, d2, h, hr,
        queries, grad_output, key_proj, value_proj,
        queries, grad_output, key_proj, value_proj,
        *outs,
    )


def place_kernel(ids_refs, rows_ref, out_ref):
    me = lax.axis_index("tp")
    tp_size = len(ids_refs)
    owned, taps = out_ref.shape
    slices, _, each, _ = rows_ref.shape
    total = jnp.zeros(out_ref.shape, WIDE)
    for k in range(tp_size):
        source = lax.rem(me + tp_size - k, tp_size)
        ids = ids_refs[k][owned : owned + 16, :].astype(WIDE)
        number = (ids[0:1, :] * 256.0 + ids[1:2, :]).astype(jnp.int32)
        here = number.shape[1]
        slot = lax.broadcasted_iota(jnp.int32, (owned, here), 0) + me * owned
        chosen = (slot == number).astype(WIDE).astype(NARROW)
        piece = rows_ref[:, pl.ds(source, 1)].reshape(slices * each, taps)
        total = total + wide_dot(chosen, piece, 1, 0)
    row = lax.broadcasted_iota(jnp.int32, (taps, taps), 0)
    lane = lax.broadcasted_iota(jnp.int32, (taps, taps), 1)
    turn = (lax.rem(row + lane, taps) == 0).astype(WIDE).astype(NARROW)
    out_ref[...] = wide_dot(total.astype(NARROW), turn, 1, 0)


def shards(queries, key_proj, value_proj, grad_output, filters, group_of):
    windows, channels, positions = queries.shape
    owned, taps = filters.shape
    ctx_size, tp_size, dp_size = (lax.axis_size(a) for a in ("ctx", "tp", "dp"))
    members = channels // owned
    half = windows // 2
    even = lax.rem(lax.axis_index("ctx"), 2) == 0

    u_ends = key_proj[:half, :, -taps:] * value_proj[:half, :, -taps:]
    d_ends = queries[half:, :, :taps] * grad_output[half:, :, :taps]
    every = range(ctx_size)
    near = [(i, i ^ 1) for i in every]
    far = [(i, i + 1) for i in every if i % 2 == 1 and i + 1 < ctx_size]
    far += [(i, i - 1) for i in every if i % 2 == 0 and i > 0]
    x1 = lax.ppermute(jnp.where(even, u_ends, d_ends), "ctx", near)
    d1 = lax.ppermute(jnp.where(even, d_ends, u_ends), "ctx", far)

    run_ids = group_of.reshape(1, owned, members)[:, :, 0]
    id_rows = jnp.concatenate(
        [run_ids // 256, run_ids % 256, jnp.zeros((14, owned), jnp.int32)], axis=0
    ).astype(NARROW)
    sent = jnp.concatenate([filters.astype(NARROW), id_rows], axis=0)
    heard = [sent]
    for k in range(1, tp_size):
        heard.append(lax.ppermute(sent, "tp", [(i, (i + k) % tp_size) for i in range(tp_size)]))

    *outs, h, hr, near_2, far_2 = conv(
        run_ids, heard, owned, queries, key_proj, value_proj, grad_output, members
    )
    x2 = lax.ppermute(near_2, "ctx", near)
    d2 = lax.ppermute(far_2, "ctx", far)
    scale = 1.0 / (windows * positions * dp_size * ctx_size)
    grad = outer_terms(x1, d1, h, queries, key_proj, value_proj, grad_output, members, scale)
    outs = border(x1, d1, x2, d2, h, hr, queries, key_proj, value_proj, grad_output, outs, members)

    slices = dp_size * ctx_size
    each = owned // slices
    swapped = lax.all_to_all(grad, ("dp", "ctx"), 0, 0, tiled=True)
    summed = jnp.sum(swapped.reshape(slices, each, taps), axis=0).astype(NARROW)
    copies = jnp.broadcast_to(summed[None], (slices * tp_size, each, taps))
    rows = lax.all_to_all(copies, ("dp", "ctx", "tp"), 0, 0, tiled=True)
    rows = rows.reshape(slices, tp_size, each, taps)

    def kernel(*refs):
        place_kernel(refs[:tp_size], refs[tp_size], refs[tp_size + 2])

    grad_filters = pl.pallas_call(
        kernel,
        in_specs=[pl.BlockSpec(memory_space=pltpu.VMEM)] * (tp_size + 1)
        + [pl.BlockSpec(memory_space=pl.ANY)],
        out_specs=pl.BlockSpec(memory_space=pltpu.VMEM),
        out_shape=jax.ShapeDtypeStruct((owned, taps), WIDE),
        name="place",
    )(*heard, rows, outs[0])
    return (*outs, grad_filters)


def solution(mesh):
    data = P("dp", "tp", "ctx")
    in_specs = (data, data, data, data, P("tp", None), P("tp"))
    out_specs = (data, data, data, data, P("tp", None))
    return jax.shard_map(shards, mesh=mesh, in_specs=in_specs, out_specs=out_specs, check_vma=False)
```

```python
import jax
import jax.numpy as jnp
from jax import lax
from jax.experimental import pallas as pl
from jax.experimental.pallas import tpu as pltpu
from jax.sharding import PartitionSpec as P


WIDE = jnp.float32
NARROW = jnp.bfloat16


def wide_dot(left, right, left_dim, right_dim):
    return lax.dot_general(
        left, right, (((left_dim,), (right_dim,)), ((), ())), preferred_element_type=WIDE
    )


def circulant(filter_row):
    taps = filter_row.shape[1]
    spread = jnp.broadcast_to(filter_row, (taps, taps))
    return pltpu.roll(spread, 0, 1, stride=1, stride_axis=0)


def band_weights(h_row, hr_row):
    taps = h_row.shape[1]
    row = lax.broadcasted_iota(jnp.int32, (taps, taps), 0)
    lane = lax.broadcasted_iota(jnp.int32, (taps, taps), 1)
    turned = circulant(h_row)
    own = jnp.where(lane >= row, turned, 0.0).astype(NARROW)
    earlier = jnp.where(lane >= row, 0.0, turned).astype(NARROW)
    turned = circulant(hr_row)
    own_back = jnp.where(lane <= row, turned, 0.0).astype(NARROW)
    later = jnp.where(lane <= row, 0.0, turned).astype(NARROW)
    return jnp.concatenate([earlier, own], axis=0), jnp.concatenate([own_back, later], axis=0)


def diagonal_sum(square):
    taps = square.shape[0]
    total = square[:8]
    for a in range(8, taps, 8):
        total = total + pltpu.roll(square[a : a + 8], taps - a, 1)
    row = lax.broadcasted_iota(jnp.int32, total.shape, 0)
    for bit in (1, 2, 4):
        total = jnp.where(row & bit != 0, pltpu.roll(total, taps - bit, 1), total)
    return jnp.sum(total, axis=0, keepdims=True)


def conv_kernel(tp_size, owned, members, ids_ref, *refs):
    pieces = refs[:tp_size]
    q_ref, k_ref, v_ref, g_ref = refs[tp_size : tp_size + 4]
    gated_ref, gq_ref, gk_ref, gv_ref, h_ref, hr_ref, u_all, d_all = refs[tp_size + 4 :]
    taps = h_ref.shape[1]
    windows, channels, positions = q_ref.shape
    blocks = positions // taps
    step = pl.program_id(0)

    @pl.when(step == 0)
    def _():
        me = lax.axis_index("tp")
        group = lax.broadcasted_iota(jnp.int32, (owned, h_ref.shape[0]), 0)
        total = jnp.zeros(h_ref.shape, WIDE)
        for k in range(tp_size):
            source = lax.rem(me + tp_size - k, tp_size)
            chosen = (group + source * owned == ids_ref[...]).astype(WIDE).astype(NARROW)
            total = total + wide_dot(chosen, pieces[k][:owned, :], 0, 0)
        h_ref[...] = total
        row = lax.broadcasted_iota(jnp.int32, (taps, taps), 0)
        lane = lax.broadcasted_iota(jnp.int32, (taps, taps), 1)
        turn = (lax.rem(row + lane, taps) == 0).astype(WIDE).astype(NARROW)
        hr_ref[...] = wide_dot(total.astype(NARROW), turn, 1, 0)

    groups = channels // members
    for r in range(groups):
        rows = slice(r * members, (r + 1) * members)
        at = step * groups + r
        all_rows = pl.ds(pl.multiple_of(at * members, members), members)
        forward, backward = band_weights(h_ref[pl.ds(at, 1), :], hr_ref[pl.ds(at, 1), :])
        z_in, du_in = [], []
        for w in range(windows):
            u = k_ref[w, rows, :] * v_ref[w, rows, :]
            d = q_ref[w, rows, :] * g_ref[w, rows, :]
            u_all[w, all_rows, :] = u
            d_all[w, all_rows, :] = d
            for b in range(1, blocks):
                z_in.append(u[:, (b - 1) * taps : (b + 1) * taps])
                du_in.append(d[:, (b - 1) * taps : (b + 1) * taps])
        z = wide_dot(jnp.concatenate(z_in, axis=0), forward, 1, 0).astype(NARROW)
        du = wide_dot(jnp.concatenate(du_in, axis=0), backward, 1, 0).astype(NARROW)
        at = 0
        for w in range(windows):
            for b in range(1, blocks):
                cols = slice(b * taps, (b + 1) * taps)
                part = z[at * members : (at + 1) * members]
                gated_ref[w, rows, cols] = q_ref[w, rows, cols] * part
                gq_ref[w, rows, cols] = g_ref[w, rows, cols] * part
                cols = slice((b - 1) * taps, b * taps)
                part = du[at * members : (at + 1) * members]
                gk_ref[w, rows, cols] = v_ref[w, rows, cols] * part
                gv_ref[w, rows, cols] = k_ref[w, rows, cols] * part
                at += 1


def on_chip(arrays):
    return [pltpu.with_memory_space_constraint(a, pltpu.VMEM) for a in arrays]


def off_chip(arrays):
    return [pltpu.with_memory_space_constraint(a, pltpu.HBM) for a in arrays]


def whole_spec(shape):
    return pl.BlockSpec(shape, lambda i: (0,) * len(shape))


def conv(ids, heard, owned, queries, key_proj, value_proj, grad_output, members, step_groups=32):
    windows, channels, positions = queries.shape
    taps = heard[0].shape[1]
    here = channels // members
    block = step_groups * members
    vmem = pl.BlockSpec(memory_space=pltpu.VMEM)
    wide_spec = pl.BlockSpec((windows, block, positions), lambda i: (0, i, 0))
    big = jax.ShapeDtypeStruct(queries.shape, NARROW)
    table = jax.ShapeDtypeStruct((here, taps), WIDE)

    def kernel(*refs):
        conv_kernel(len(heard), owned, members, *refs)

    return pl.pallas_call(
        kernel,
        grid=(channels // block,),
        in_specs=[vmem] * (1 + len(heard)) + [wide_spec] * 4,
        out_specs=[wide_spec] * 4 + [whole_spec(table.shape)] * 2 + [vmem] * 2,
        out_shape=[big] * 4 + [table] * 2 + [pltpu.VMEM(big.shape, NARROW)] * 2,
        cost_estimate=pl.CostEstimate(
            flops=8 * taps * queries.size, bytes_accessed=16 * queries.size, transcendentals=0
        ),
        compiler_params=pltpu.CompilerParams(vmem_limit_bytes=40000000),
        name="conv",
    )(ids, *on_chip(heard), *off_chip((queries, key_proj, value_proj, grad_output)))


def outer_kernel(members, scale, chunk, x_ref, d_ref, u_all, d_all, out_ref, square_ref):
    even = lax.rem(lax.axis_index("ctx"), 2) == 0
    windows, _, positions = u_all.shape
    channels = out_ref.shape[0] * members
    half = windows // 2
    taps = x_ref.shape[-1]
    first = pl.program_id(0) * channels
    blocks = positions // taps
    chunks = channels // members // chunk
    slots = square_ref.shape[0]
    row = lax.broadcasted_iota(jnp.int32, (taps, taps), 0)
    lane = lax.broadcasted_iota(jnp.int32, (taps, taps), 1)
    empty = jnp.zeros((members, taps), NARROW)

    def squares(at, slot):
        for r in range(chunk):
            rows = pl.ds(pl.multiple_of(first + (at * chunk + r) * members, members), members)
            lefts, rights = [], []
            for w in range(windows):
                u = u_all[w, rows, :]
                d = d_all[w, rows, :]
                if w < half:
                    prior = jnp.where(even, d_ref[w, rows, :], x_ref[w, rows, :])
                else:
                    prior = empty
                    lefts.append(
                        jnp.where(even, x_ref[w - half, rows, :], d_ref[w - half, rows, :])
                    )
                    rights.append(jnp.concatenate([u[:, -taps:], empty], axis=1))
                for b in range(blocks):
                    lefts.append(d[:, b * taps : (b + 1) * taps])
                    if b == 0:
                        rights.append(jnp.concatenate([prior, u[:, :taps]], axis=1))
                    else:
                        rights.append(u[:, (b - 1) * taps : (b + 1) * taps])
            outer = wide_dot(jnp.concatenate(lefts, axis=0), jnp.concatenate(rights, axis=0), 0, 0)
            square_ref[slot, r] = jnp.where(lane <= row, outer[:, taps:], outer[:, :taps])

    def sums(at, slot):
        found = [diagonal_sum(square_ref[slot, r]) for r in range(chunk)]
        out_ref[at * chunk : (at + 1) * chunk, :] = jnp.concatenate(found, axis=0) * scale

    for at in range(chunks + 1):
        if at < chunks:
            squares(at, at % slots)
        if at > 0:
            sums(at - 1, (at - 1) % slots)


def outer_terms(x1, d1, u, d, members, scale, step_groups=16, chunk=8, slots=2):
    channels = u.shape[1]
    taps = x1.shape[-1]
    block = step_groups * members
    vmem = pl.BlockSpec(memory_space=pltpu.VMEM)

    def kernel(*refs):
        outer_kernel(members, scale, chunk, *refs)

    return pl.pallas_call(
        kernel,
        grid=(channels // block,),
        in_specs=[vmem] * 4,
        out_specs=pl.BlockSpec((step_groups, taps), lambda i: (i, 0)),
        out_shape=jax.ShapeDtypeStruct((channels // members, taps), WIDE),
        scratch_shapes=[pltpu.VMEM((slots, chunk, taps, taps), WIDE)],
        cost_estimate=pl.CostEstimate(
            flops=8 * taps * u.size, bytes_accessed=8 * u.size, transcendentals=0
        ),
        compiler_params=pltpu.CompilerParams(vmem_limit_bytes=20000000),
        name="outer",
    )(*on_chip((x1, d1, u, d)))


def border_kernel(members, *refs):
    x1_ref, d1_ref, x2_ref, d2_ref, u_all, h_ref, hr_ref = refs[:7]
    qh_ref, gh_ref, qt_ref, gt_ref, kt_ref, vt_ref = refs[7:13]
    gated_ref, gq_ref, gk_ref, gv_ref = refs[17:]
    even = lax.rem(lax.axis_index("ctx"), 2) == 0
    half, _, taps = x1_ref.shape
    channels = qh_ref.shape[1]
    start = pl.program_id(0) * channels
    for r in range(channels // members):
        rows = slice(r * members, (r + 1) * members)
        halo_rows = pl.ds(pl.multiple_of(start + r * members, members), members)
        forward, backward = band_weights(h_ref[r : r + 1, :], hr_ref[r : r + 1, :])
        z_in, du_in = [], []
        for w in range(2 * half):
            first = w < half
            x = (x1_ref if first else x2_ref)[w % half, rows, :]
            d = (d1_ref if first else d2_ref)[w % half, rows, :]
            z_in.append(
                jnp.concatenate([jnp.where(even, d, x), u_all[w, halo_rows, :taps]], axis=1)
            )
            x = (x2_ref if first else x1_ref)[w % half, rows, :]
            d = (d2_ref if first else d1_ref)[w % half, rows, :]
            du_in.append(
                jnp.concatenate([qt_ref[w, rows, :] * gt_ref[w, rows, :], jnp.where(even, x, d)], axis=1)
            )
        z = wide_dot(jnp.concatenate(z_in, axis=0), forward, 1, 0).astype(NARROW)
        du = wide_dot(jnp.concatenate(du_in, axis=0), backward, 1, 0).astype(NARROW)
        for w in range(2 * half):
            part = z[w * members : (w + 1) * members]
            gated_ref[w, rows, :] = qh_ref[w, rows, :] * part
            gq_ref[w, rows, :] = gh_ref[w, rows, :] * part
            part = du[w * members : (w + 1) * members]
            gk_ref[w, rows, :] = vt_ref[w, rows, :] * part
            gv_ref[w, rows, :] = kt_ref[w, rows, :] * part


def border(x1, d1, x2, d2, u, h, hr, queries, key_proj, value_proj, grad_output, outs, members, step_groups=64):
    windows, channels, positions = queries.shape
    taps = x1.shape[-1]
    block = step_groups * members
    last = positions // taps - 1
    halo = pl.BlockSpec((x1.shape[0], block, taps), lambda i: (0, i, 0))
    vmem = pl.BlockSpec(memory_space=pltpu.VMEM)
    head = pl.BlockSpec((windows, block, taps), lambda i: (0, i, 0))
    tail = pl.BlockSpec((windows, block, taps), lambda i: (0, i, last))
    rows = pl.BlockSpec((step_groups, taps), lambda i: (i, 0))
    anywhere = pl.BlockSpec(memory_space=pltpu.HBM)

    def kernel(*refs):
        border_kernel(members, *refs)

    return pl.pallas_call(
        kernel,
        grid=(channels // block,),
        in_specs=[halo] * 4 + [vmem] + [rows] * 2 + [head] * 2 + [tail] * 4 + [anywhere] * 4,
        out_specs=[head, head, tail, tail],
        out_shape=[jax.ShapeDtypeStruct(queries.shape, NARROW)] * 4,
        input_output_aliases={13: 0, 14: 1, 15: 2, 16: 3},
        cost_estimate=pl.CostEstimate(
            flops=32 * taps * x1.size, bytes_accessed=64 * x1.size, transcendentals=0
        ),
        compiler_params=pltpu.CompilerParams(vmem_limit_bytes=40000000),
        name="border",
    )(
        *off_chip((x1, d1, x2, d2)),
        *on_chip((u,)),
        h,
        hr,
        *off_chip((queries, grad_output, queries, grad_output, key_proj, value_proj, *outs)),
    )


def place_kernel(ids_refs, rows_ref, out_ref):
    me = lax.axis_index("tp")
    tp_size = len(ids_refs)
    owned, taps = out_ref.shape
    slices, _, each, _ = rows_ref.shape
    total = jnp.zeros(out_ref.shape, WIDE)
    for k in range(tp_size):
        source = lax.rem(me + tp_size - k, tp_size)
        ids = ids_refs[k][owned : owned + 16, :].astype(WIDE)
        number = (ids[0:1, :] * 256.0 + ids[1:2, :]).astype(jnp.int32)
        here = number.shape[1]
        slot = lax.broadcasted_iota(jnp.int32, (owned, here), 0) + me * owned
        chosen = (slot == number).astype(WIDE).astype(NARROW)
        piece = rows_ref[:, pl.ds(source, 1)].reshape(slices * each, taps)
        total = total + wide_dot(chosen, piece, 1, 0)
    row = lax.broadcasted_iota(jnp.int32, (taps, taps), 0)
    lane = lax.broadcasted_iota(jnp.int32, (taps, taps), 1)
    turn = (lax.rem(row + lane, taps) == 0).astype(WIDE).astype(NARROW)
    out_ref[...] = wide_dot(total.astype(NARROW), turn, 1, 0)


def shards(queries, key_proj, value_proj, grad_output, filters, group_of):
    windows, channels, positions = queries.shape
    owned, taps = filters.shape
    ctx_size, tp_size, dp_size = (lax.axis_size(a) for a in ("ctx", "tp", "dp"))
    members = channels // owned
    half = windows // 2
    even = lax.rem(lax.axis_index("ctx"), 2) == 0

    def messages(streams, u_at, d_at):
        q, k, v, g = streams
        u = k[u_at : u_at + half, :, -taps:] * v[u_at : u_at + half, :, -taps:]
        d = q[d_at : d_at + half, :, :taps] * g[d_at : d_at + half, :, :taps]
        return jnp.where(even, u, d), jnp.where(even, d, u)

    every = range(ctx_size)
    near = [(i, i ^ 1) for i in every]
    far = [(i, i + 1) for i in every if i % 2 == 1 and i + 1 < ctx_size]
    far += [(i, i - 1) for i in every if i % 2 == 0 and i > 0]

    streams = (queries, key_proj, value_proj, grad_output)
    near_1, far_1 = messages(streams, 0, half)
    x1 = lax.ppermute(near_1, "ctx", near)
    d1 = lax.ppermute(far_1, "ctx", far)

    run_ids = group_of.reshape(1, owned, members)[:, :, 0]
    id_rows = jnp.concatenate(
        [run_ids // 256, run_ids % 256, jnp.zeros((14, owned), jnp.int32)], axis=0
    ).astype(NARROW)
    sent = jnp.concatenate([filters.astype(NARROW), id_rows], axis=0)
    heard = [sent]
    for k in range(1, tp_size):
        pairs = [(i, (i + k) % tp_size) for i in range(tp_size)]
        heard.append(lax.ppermute(sent, "tp", pairs))

    *streams_2, _ = lax.optimization_barrier((*streams, near_1))
    near_2, far_2 = messages(streams_2, half, 0)
    x2 = lax.ppermute(near_2, "ctx", near)
    d2 = lax.ppermute(far_2, "ctx", far)

    *outs, h, hr, u, d = conv(
        run_ids, heard, owned, queries, key_proj, value_proj, grad_output, members
    )
    scale = 1.0 / (windows * positions * dp_size * ctx_size)
    grad = outer_terms(x1, d1, u, d, members, scale)
    outs = border(x1, d1, x2, d2, u, h, hr, queries, key_proj, value_proj, grad_output, outs, members)

    slices = dp_size * ctx_size
    each = owned // slices
    swapped = lax.all_to_all(grad, ("dp", "ctx"), 0, 0, tiled=True)
    summed = jnp.sum(swapped.reshape(slices, each, taps), axis=0).astype(NARROW)
    copies = jnp.broadcast_to(summed[None], (slices * tp_size, each, taps))
    rows = lax.all_to_all(copies, ("dp", "ctx", "tp"), 0, 0, tiled=True)
    rows = rows.reshape(slices, tp_size, each, taps)

    def kernel(*refs):
        place_kernel(refs[:tp_size], refs[tp_size], refs[tp_size + 1])

    grad_filters = pl.pallas_call(
        kernel,
        in_specs=[pl.BlockSpec(memory_space=pltpu.VMEM)] * (tp_size + 1),
        out_specs=pl.BlockSpec(memory_space=pltpu.VMEM),
        out_shape=jax.ShapeDtypeStruct((owned, taps), WIDE),
        compiler_params=pltpu.CompilerParams(vmem_limit_bytes=10000000),
        name="place",
    )(*on_chip((*heard, rows)))
    return (*outs, grad_filters)


def solution(mesh):
    data = P("dp", "tp", "ctx")
    in_specs = (data, data, data, data, P("tp", None), P("tp"))
    out_specs = (data, data, data, data, P("tp", None))

    return jax.shard_map(shards, mesh=mesh, in_specs=in_specs, out_specs=out_specs, check_vma=False)
```

```python
import jax
import jax.numpy as jnp
from jax import lax
from jax.experimental import pallas as pl
from jax.experimental.pallas import tpu as pltpu
from jax.sharding import PartitionSpec as P


WIDE = jnp.float32
NARROW = jnp.bfloat16


def wide_dot(left, right, left_dim, right_dim):
    return lax.dot_general(
        left, right, (((left_dim,), (right_dim,)), ((), ())), preferred_element_type=WIDE
    )


def circulant(filter_row):
    taps = filter_row.shape[1]
    spread = jnp.broadcast_to(filter_row, (taps, taps))
    return pltpu.roll(spread, 0, 1, stride=1, stride_axis=0)


def band_weights(h_row, hr_row):
    taps = h_row.shape[1]
    row = lax.broadcasted_iota(jnp.int32, (taps, taps), 0)
    lane = lax.broadcasted_iota(jnp.int32, (taps, taps), 1)
    turned = circulant(h_row)
    own = jnp.where(lane >= row, turned, 0.0).astype(NARROW)
    earlier = jnp.where(lane >= row, 0.0, turned).astype(NARROW)
    turned = circulant(hr_row)
    own_back = jnp.where(lane <= row, turned, 0.0).astype(NARROW)
    later = jnp.where(lane <= row, 0.0, turned).astype(NARROW)
    return jnp.concatenate([earlier, own], axis=0), jnp.concatenate([own_back, later], axis=0)


def diagonal_sum(square):
    taps = square.shape[0]
    total = square[:8]
    for a in range(8, taps, 8):
        total = total + pltpu.roll(square[a : a + 8], taps - a, 1)
    row = lax.broadcasted_iota(jnp.int32, total.shape, 0)
    for bit in (1, 2, 4):
        total = jnp.where(row & bit != 0, pltpu.roll(total, taps - bit, 1), total)
    return jnp.sum(total, axis=0, keepdims=True)


def conv_kernel(tp_size, owned, members, ids_ref, *refs):
    pieces = refs[:tp_size]
    q_ref, k_ref, v_ref, g_ref = refs[tp_size : tp_size + 4]
    gated_ref, gq_ref, gk_ref, gv_ref, h_ref, hr_ref, u_all, d_all = refs[tp_size + 4 :]
    taps = h_ref.shape[1]
    windows, channels, positions = q_ref.shape
    blocks = positions // taps
    step = pl.program_id(0)

    @pl.when(step == 0)
    def _():
        me = lax.axis_index("tp")
        group = lax.broadcasted_iota(jnp.int32, (owned, h_ref.shape[0]), 0)
        total = jnp.zeros(h_ref.shape, WIDE)
        for k in range(tp_size):
            source = lax.rem(me + tp_size - k, tp_size)
            chosen = (group + source * owned == ids_ref[...]).astype(WIDE).astype(NARROW)
            total = total + wide_dot(chosen, pieces[k][:owned, :], 0, 0)
        h_ref[...] = total
        row = lax.broadcasted_iota(jnp.int32, (taps, taps), 0)
        lane = lax.broadcasted_iota(jnp.int32, (taps, taps), 1)
        turn = (lax.rem(row + lane, taps) == 0).astype(WIDE).astype(NARROW)
        hr_ref[...] = wide_dot(total.astype(NARROW), turn, 1, 0)

    groups = channels // members
    for r in range(groups):
        rows = slice(r * members, (r + 1) * members)
        at = step * groups + r
        all_rows = pl.ds(pl.multiple_of(at * members, members), members)
        forward, backward = band_weights(h_ref[pl.ds(at, 1), :], hr_ref[pl.ds(at, 1), :])
        z_in, du_in = [], []
        for w in range(windows):
            u = k_ref[w, rows, :] * v_ref[w, rows, :]
            d = q_ref[w, rows, :] * g_ref[w, rows, :]
            u_all[w, all_rows, :] = u
            d_all[w, all_rows, :] = d
            for b in range(1, blocks):
                z_in.append(u[:, (b - 1) * taps : (b + 1) * taps])
                du_in.append(d[:, (b - 1) * taps : (b + 1) * taps])
        z = wide_dot(jnp.concatenate(z_in, axis=0), forward, 1, 0).astype(NARROW)
        du = wide_dot(jnp.concatenate(du_in, axis=0), backward, 1, 0).astype(NARROW)
        at = 0
        for w in range(windows):
            for b in range(1, blocks):
                cols = slice(b * taps, (b + 1) * taps)
                part = z[at * members : (at + 1) * members]
                gated_ref[w, rows, cols] = q_ref[w, rows, cols] * part
                gq_ref[w, rows, cols] = g_ref[w, rows, cols] * part
                cols = slice((b - 1) * taps, b * taps)
                part = du[at * members : (at + 1) * members]
                gk_ref[w, rows, cols] = v_ref[w, rows, cols] * part
                gv_ref[w, rows, cols] = k_ref[w, rows, cols] * part
                at += 1


def on_chip(arrays):
    return [pltpu.with_memory_space_constraint(a, pltpu.VMEM) for a in arrays]


def off_chip(arrays):
    return [pltpu.with_memory_space_constraint(a, pltpu.HBM) for a in arrays]


def whole_spec(shape):
    return pl.BlockSpec(shape, lambda i: (0,) * len(shape))


def conv(ids, heard, owned, queries, key_proj, value_proj, grad_output, members, step_groups=32):
    windows, channels, positions = queries.shape
    taps = heard[0].shape[1]
    here = channels // members
    block = step_groups * members
    vmem = pl.BlockSpec(memory_space=pltpu.VMEM)
    wide_spec = pl.BlockSpec((windows, block, positions), lambda i: (0, i, 0))
    big = jax.ShapeDtypeStruct(queries.shape, NARROW)
    table = jax.ShapeDtypeStruct((here, taps), WIDE)

    def kernel(*refs):
        conv_kernel(len(heard), owned, members, *refs)

    return pl.pallas_call(
        kernel,
        grid=(channels // block,),
        in_specs=[vmem] * (1 + len(heard)) + [wide_spec] * 4,
        out_specs=[wide_spec] * 4 + [whole_spec(table.shape)] * 2 + [vmem] * 2,
        out_shape=[big] * 4 + [table] * 2 + [pltpu.VMEM(big.shape, NARROW)] * 2,
        cost_estimate=pl.CostEstimate(
            flops=8 * taps * queries.size, bytes_accessed=16 * queries.size, transcendentals=0
        ),
        compiler_params=pltpu.CompilerParams(vmem_limit_bytes=40000000),
        name="conv",
    )(ids, *on_chip(heard), *off_chip((queries, key_proj, value_proj, grad_output)))


def outer_kernel(members, scale, chunk, x_ref, d_ref, u_all, d_all, out_ref, square_ref):
    even = lax.rem(lax.axis_index("ctx"), 2) == 0
    windows, _, positions = u_all.shape
    channels = out_ref.shape[0] * members
    half = windows // 2
    taps = x_ref.shape[-1]
    first = pl.program_id(0) * channels
    blocks = positions // taps
    chunks = channels // members // chunk
    slots = square_ref.shape[0]
    row = lax.broadcasted_iota(jnp.int32, (taps, taps), 0)
    lane = lax.broadcasted_iota(jnp.int32, (taps, taps), 1)
    empty = jnp.zeros((members, taps), NARROW)

    def squares(at, slot):
        for r in range(chunk):
            rows = pl.ds(pl.multiple_of(first + (at * chunk + r) * members, members), members)
            lefts, rights = [], []
            for w in range(windows):
                u = u_all[w, rows, :]
                d = d_all[w, rows, :]
                if w < half:
                    prior = jnp.where(even, d_ref[w, rows, :], x_ref[w, rows, :])
                else:
                    prior = empty
                    lefts.append(
                        jnp.where(even, x_ref[w - half, rows, :], d_ref[w - half, rows, :])
                    )
                    rights.append(jnp.concatenate([u[:, -taps:], empty], axis=1))
                for b in range(blocks):
                    lefts.append(d[:, b * taps : (b + 1) * taps])
                    if b == 0:
                        rights.append(jnp.concatenate([prior, u[:, :taps]], axis=1))
                    else:
                        rights.append(u[:, (b - 1) * taps : (b + 1) * taps])
            outer = wide_dot(jnp.concatenate(lefts, axis=0), jnp.concatenate(rights, axis=0), 0, 0)
            square_ref[slot, r] = jnp.where(lane <= row, outer[:, taps:], outer[:, :taps])

    def sums(at, slot):
        found = [diagonal_sum(square_ref[slot, r]) for r in range(chunk)]
        out_ref[at * chunk : (at + 1) * chunk, :] = jnp.concatenate(found, axis=0) * scale

    for at in range(chunks + 1):
        if at < chunks:
            squares(at, at % slots)
        if at > 0:
            sums(at - 1, (at - 1) % slots)


def outer_terms(x1, d1, u, d, members, scale, step_groups=16, chunk=8, slots=2):
    channels = u.shape[1]
    taps = x1.shape[-1]
    block = step_groups * members
    vmem = pl.BlockSpec(memory_space=pltpu.VMEM)

    def kernel(*refs):
        outer_kernel(members, scale, chunk, *refs)

    return pl.pallas_call(
        kernel,
        grid=(channels // block,),
        in_specs=[vmem] * 4,
        out_specs=pl.BlockSpec((step_groups, taps), lambda i: (i, 0)),
        out_shape=jax.ShapeDtypeStruct((channels // members, taps), WIDE),
        scratch_shapes=[pltpu.VMEM((slots, chunk, taps, taps), WIDE)],
        cost_estimate=pl.CostEstimate(
            flops=8 * taps * u.size, bytes_accessed=8 * u.size, transcendentals=0
        ),
        compiler_params=pltpu.CompilerParams(vmem_limit_bytes=20000000),
        name="outer",
    )(*on_chip((x1, d1, u, d)))


def border_kernel(members, *refs):
    x1_ref, d1_ref, x2_ref, d2_ref, u_all, h_ref, hr_ref = refs[:7]
    qh_ref, gh_ref, qt_ref, gt_ref, kt_ref, vt_ref = refs[7:13]
    gated_ref, gq_ref, gk_ref, gv_ref = refs[17:]
    even = lax.rem(lax.axis_index("ctx"), 2) == 0
    half, _, taps = x1_ref.shape
    channels = qh_ref.shape[1]
    start = pl.program_id(0) * channels
    for r in range(channels // members):
        rows = slice(r * members, (r + 1) * members)
        halo_rows = pl.ds(pl.multiple_of(start + r * members, members), members)
        forward, backward = band_weights(h_ref[r : r + 1, :], hr_ref[r : r + 1, :])
        z_in, du_in = [], []
        for w in range(2 * half):
            first = w < half
            x = (x1_ref if first else x2_ref)[w % half, rows, :]
            d = (d1_ref if first else d2_ref)[w % half, rows, :]
            z_in.append(
                jnp.concatenate([jnp.where(even, d, x), u_all[w, halo_rows, :taps]], axis=1)
            )
            x = (x2_ref if first else x1_ref)[w % half, rows, :]
            d = (d2_ref if first else d1_ref)[w % half, rows, :]
            du_in.append(
                jnp.concatenate([qt_ref[w, rows, :] * gt_ref[w, rows, :], jnp.where(even, x, d)], axis=1)
            )
        z = wide_dot(jnp.concatenate(z_in, axis=0), forward, 1, 0).astype(NARROW)
        du = wide_dot(jnp.concatenate(du_in, axis=0), backward, 1, 0).astype(NARROW)
        for w in range(2 * half):
            part = z[w * members : (w + 1) * members]
            gated_ref[w, rows, :] = qh_ref[w, rows, :] * part
            gq_ref[w, rows, :] = gh_ref[w, rows, :] * part
            part = du[w * members : (w + 1) * members]
            gk_ref[w, rows, :] = vt_ref[w, rows, :] * part
            gv_ref[w, rows, :] = kt_ref[w, rows, :] * part


def border(x1, d1, x2, d2, u, h, hr, queries, key_proj, value_proj, grad_output, outs, members, step_groups=64):
    windows, channels, positions = queries.shape
    taps = x1.shape[-1]
    block = step_groups * members
    last = positions // taps - 1
    halo = pl.BlockSpec((x1.shape[0], block, taps), lambda i: (0, i, 0))
    vmem = pl.BlockSpec(memory_space=pltpu.VMEM)
    head = pl.BlockSpec((windows, block, taps), lambda i: (0, i, 0))
    tail = pl.BlockSpec((windows, block, taps), lambda i: (0, i, last))
    rows = pl.BlockSpec((step_groups, taps), lambda i: (i, 0))
    anywhere = pl.BlockSpec(memory_space=pltpu.HBM)

    def kernel(*refs):
        border_kernel(members, *refs)

    return pl.pallas_call(
        kernel,
        grid=(channels // block,),
        in_specs=[halo] * 4 + [vmem] + [rows] * 2 + [head] * 2 + [tail] * 4 + [anywhere] * 4,
        out_specs=[head, head, tail, tail],
        out_shape=[jax.ShapeDtypeStruct(queries.shape, NARROW)] * 4,
        input_output_aliases={13: 0, 14: 1, 15: 2, 16: 3},
        cost_estimate=pl.CostEstimate(
            flops=32 * taps * x1.size, bytes_accessed=64 * x1.size, transcendentals=0
        ),
        compiler_params=pltpu.CompilerParams(vmem_limit_bytes=40000000),
        name="border",
    )(
        *off_chip((x1, d1, x2, d2)),
        *on_chip((u,)),
        h,
        hr,
        *off_chip((queries, grad_output, queries, grad_output, key_proj, value_proj, *outs)),
    )


def place_kernel(ids_refs, rows_ref, out_ref):
    me = lax.axis_index("tp")
    tp_size = len(ids_refs)
    owned, taps = out_ref.shape
    slices, _, each, _ = rows_ref.shape
    total = jnp.zeros(out_ref.shape, WIDE)
    for k in range(tp_size):
        source = lax.rem(me + tp_size - k, tp_size)
        ids = ids_refs[k][owned : owned + 16, :].astype(WIDE)
        number = (ids[0:1, :] * 256.0 + ids[1:2, :]).astype(jnp.int32)
        here = number.shape[1]
        slot = lax.broadcasted_iota(jnp.int32, (owned, here), 0) + me * owned
        chosen = (slot == number).astype(WIDE).astype(NARROW)
        piece = rows_ref[:, pl.ds(source, 1)].reshape(slices * each, taps)
        total = total + wide_dot(chosen, piece, 1, 0)
    row = lax.broadcasted_iota(jnp.int32, (taps, taps), 0)
    lane = lax.broadcasted_iota(jnp.int32, (taps, taps), 1)
    turn = (lax.rem(row + lane, taps) == 0).astype(WIDE).astype(NARROW)
    out_ref[...] = wide_dot(total.astype(NARROW), turn, 1, 0)


def shards(queries, key_proj, value_proj, grad_output, filters, group_of):
    windows, channels, positions = queries.shape
    owned, taps = filters.shape
    ctx_size, tp_size, dp_size = (lax.axis_size(a) for a in ("ctx", "tp", "dp"))
    members = channels // owned
    half = windows // 2
    even = lax.rem(lax.axis_index("ctx"), 2) == 0

    def messages(streams, u_at, d_at):
        q, k, v, g = streams
        u = k[u_at : u_at + half, :, -taps:] * v[u_at : u_at + half, :, -taps:]
        d = q[d_at : d_at + half, :, :taps] * g[d_at : d_at + half, :, :taps]
        return jnp.where(even, u, d), jnp.where(even, d, u)

    every = range(ctx_size)
    near = [(i, i ^ 1) for i in every]
    far = [(i, i + 1) for i in every if i % 2 == 1 and i + 1 < ctx_size]
    far += [(i, i - 1) for i in every if i % 2 == 0 and i > 0]

    up = [i for i in every if i % 2 == 1 and i + 1 < ctx_size]
    down = [i for i in every if i % 2 == 0 and i > 0]
    out_hop = [(i, i + 2) for i in up] + [(i, i - 2) for i in down]
    back_hop = [(i + 2, i + 1) for i in up] + [(i - 2, i - 1) for i in down]

    streams = (queries, key_proj, value_proj, grad_output)
    near_1, far_1 = messages(streams, 0, half)
    x1 = lax.ppermute(near_1, "ctx", near)
    d1 = lax.ppermute(far_1, "ctx", far)

    run_ids = group_of.reshape(1, owned, members)[:, :, 0]
    id_rows = jnp.concatenate(
        [run_ids // 256, run_ids % 256, jnp.zeros((14, owned), jnp.int32)], axis=0
    ).astype(NARROW)
    sent = jnp.concatenate([filters.astype(NARROW), id_rows], axis=0)
    heard = [sent]
    for k in range(1, tp_size):
        pairs = [(i, (i + k) % tp_size) for i in range(tp_size)]
        heard.append(lax.ppermute(sent, "tp", pairs))

    *streams_2, _ = lax.optimization_barrier((*streams, near_1))
    near_2, far_2 = messages(streams_2, half, 0)
    relay = lax.ppermute(far_2, "ctx", out_hop)
    x2 = lax.ppermute(near_2, "ctx", near)
    d2 = lax.ppermute(relay, "ctx", back_hop)

    *outs, h, hr, u, d = conv(
        run_ids, heard, owned, queries, key_proj, value_proj, grad_output, members
    )
    scale = 1.0 / (windows * positions * dp_size * ctx_size)
    grad = outer_terms(x1, d1, u, d, members, scale)
    outs = border(x1, d1, x2, d2, u, h, hr, queries, key_proj, value_proj, grad_output, outs, members)

    first_heard, *outs = lax.optimization_barrier((heard[0], *outs))
    heard[0] = first_heard
    slices = dp_size * ctx_size
    each = owned // slices
    swapped = lax.all_to_all(grad, ("dp", "ctx"), 0, 0, tiled=True)
    summed = jnp.sum(swapped.reshape(slices, each, taps), axis=0).astype(NARROW)
    copies = jnp.broadcast_to(summed[None], (slices * tp_size, each, taps))
    rows = lax.all_to_all(copies, ("dp", "ctx", "tp"), 0, 0, tiled=True)
    rows = rows.reshape(slices, tp_size, each, taps)

    def kernel(*refs):
        place_kernel(refs[:tp_size], refs[tp_size], refs[tp_size + 1])

    grad_filters = pl.pallas_call(
        kernel,
        in_specs=[pl.BlockSpec(memory_space=pltpu.VMEM)] * (tp_size + 1),
        out_specs=pl.BlockSpec(memory_space=pltpu.VMEM),
        out_shape=jax.ShapeDtypeStruct((owned, taps), WIDE),
        compiler_params=pltpu.CompilerParams(vmem_limit_bytes=10000000),
        name="place",
    )(*on_chip((*heard, rows)))
    return (*outs, grad_filters)


def solution(mesh):
    data = P("dp", "tp", "ctx")
    in_specs = (data, data, data, data, P("tp", None), P("tp"))
    out_specs = (data, data, data, data, P("tp", None))

    return jax.shard_map(shards, mesh=mesh, in_specs=in_specs, out_specs=out_specs, check_vma=False)
```
